512 devices in a mesh: dom: 16 (over z), feat: 32 (over x, y, core).
Axes of the slice: x: 4, y: 4, z: 16, core: 2. Of those that a mesh axis runs over, the one named last changes fastest.
Arguments:
- node_feats: bfloat16 [1024, 65536], P('feat', 'dom'), may hold values from -6 to 6
- out_cotangent: bfloat16 [1024, 65536], P('feat', 'dom'), may hold values from -6 to 6
- weight_self: bfloat16 [1024, 1024], P('feat'), may hold values from -0.1875 to 0.1875
- weight_neigh: bfloat16 [1024, 1024], P('feat'), may hold values from -1.5 to 1.5
- out_bias: float32 [1024], P('feat'), may hold values from -3 to 3
- send_blocks: int32 [16, 16, 2], P('dom'), may hold values from 0 to 31
- tile_rows: int32 [16, 64], P('dom'), may hold values from 0 to 31
- tile_cols: int32 [16, 64], P('dom'), may hold values from 0 to 63
- tile_count: int32 [16], P('dom'), may hold values from 1 to 64, as said below
- tile_values: bfloat16 [16, 64, 128, 128], P('dom'), may hold values from 0 to 1
Outputs:
- layer_out: bfloat16 [1024, 65536], P('feat', 'dom')
- feats_grad: bfloat16 [1024, 65536], P('feat', 'dom')
- grad_self: float32 [1024, 1024], P('feat')
- grad_neigh: float32 [1024, 1024], P('feat')
- grad_bias: float32 [1024], P('feat')
The draws below stay inside these ranges and needn't reach their ends.
Inputs may be any that keep to these rules, and one draw needn't show every extreme that they name: Slots t >= tile_count[p] of tile_rows, tile_cols and tile_values are not part of the graph; some partition uses all 64 slots.
All inputs are finite; a program needn't handle non-finite values.
Results may differ from the reference program's by a relative error of at most 0.0075.
Values may be sent and summed in bfloat16 or wider, within the bound.
No kernel may reach another device: no remote copies, remote signals or barrier semaphores. Data moves between devices by JAX's collectives and lax.ppermute only.
A program may use at most 64 MiB of HBM per device.

```python
import jax
import jax.numpy as jnp
from jax import lax

D = 1024
DOUT = 1024
BLK = 128
NBLK = 32
CAP = 2
TMAX = 64
NEXT = 64
NODES = 65536
N_DOM = 16


def draw_tile_count(key, part):
    key_counts, key_heavy = jax.random.split(jax.random.fold_in(key, 17))
    counts = jax.random.randint(key_counts, (N_DOM,), max(TMAX // 8, 1), TMAX // 2 + 1)
    heavy = jax.random.randint(key_heavy, (), 0, N_DOM)
    return jnp.where(jnp.arange(N_DOM) == heavy, TMAX, counts).astype(jnp.int32)


def set_ends(values, stream_key, low, top_value):
    longest = values.shape.index(max(values.shape))
    spots = []
    for shift in (0, 1):
        where = [jax.random.randint(jax.random.fold_in(stream_key, axis), (), 0, length) for axis, length in enumerate(values.shape)]
        where[longest] = (where[longest] + shift) % values.shape[longest]
        spots.append(tuple(where))
    return values.at[spots[0]].set(low).at[spots[1]].set(top_value)


def block_scale(own_key, extent, pieces, smallest, high):
    def one(axis_at, shards_of):
        steps = jax.random.uniform(jax.random.fold_in(jax.random.fold_in(own_key, 6), axis_at), (shards_of,), jnp.float32, smallest / len(pieces), high / len(pieces))
        return jnp.repeat(jnp.exp(steps), extent[axis_at] // shards_of).reshape((-1,) + (1,) * (len(extent) - axis_at - 1))

    level = one(*pieces[0])
    for cut in pieces[1:]:
        level = level * one(*cut)
    return level


def gaussian(own_key, dims, scale, limit, shards=(), kind=jnp.bfloat16):
    result = jax.random.normal(own_key, dims, jnp.float32) * scale
    if len(shards) > 0:
        result = block_scale(own_key, dims, shards, -0.22, 0.18) * result
    return jnp.clip(result, min=-limit, max=limit).astype(kind)


def setup_inputs(seed: int = 0) -> dict:
    key_of = jax.random.split(jax.random.key(seed), 11)
    node_feats = gaussian(key_of[0], (D, NODES), 1.0, 6.0, ((0, 32), (1, 16)))
    out_cotangent = gaussian(key_of[1], (DOUT, NODES), 1.0, 6.0, ((0, 32), (1, 16)))
    weight_self = gaussian(key_of[2], (D, DOUT), D ** -0.5, 0.1875, ((0, 32),))
    weight_neigh = gaussian(key_of[3], (D, DOUT), (D // 64) ** -0.5, 1.5, ((0, 32),))
    out_bias = gaussian(key_of[4], (DOUT,), 0.5, 3.0, ((0, 32),), jnp.float32)
    send_blocks = set_ends(jax.random.randint(key_of[5], (N_DOM, N_DOM, CAP), 0, NBLK), jax.random.fold_in(key_of[5], 1), 0, NBLK - 1).astype(jnp.int32)
    tile_rows = set_ends(jax.random.randint(key_of[6], (N_DOM, TMAX), 0, NBLK), jax.random.fold_in(key_of[6], 1), 0, NBLK - 1).astype(jnp.int32)
    tile_cols = set_ends(jax.random.randint(key_of[7], (N_DOM, TMAX), 0, NEXT), jax.random.fold_in(key_of[7], 1), 0, NEXT - 1).astype(jnp.int32)
    tile_count = draw_tile_count(jax.random.fold_in(key_of[10], 71), 0)
    tile_values = jnp.clip(1.0 * jax.random.uniform(key_of[9], (N_DOM, TMAX, BLK, BLK), jnp.float32) ** block_scale(key_of[9], (N_DOM, TMAX, BLK, BLK), ((0, 16),), -0.2, 0.2), 0.0, 1.0).astype(jnp.bfloat16)
    return {"node_feats": node_feats, "out_cotangent": out_cotangent, "weight_self": weight_self, "weight_neigh": weight_neigh, "out_bias": out_bias, "send_blocks": send_blocks, "tile_rows": tile_rows, "tile_cols": tile_cols, "tile_count": tile_count, "tile_values": tile_values}


def gelu_tanh(values):
    return jax.nn.gelu(values, approximate=True)

def reference(node_feats, out_cotangent, weight_self, weight_neigh, out_bias, send_blocks, tile_rows, tile_cols, tile_count, tile_values):
    highest = lax.Precision.HIGHEST
    blocks = node_feats.reshape(D, N_DOM, NBLK, BLK)
    owner = jnp.broadcast_to(jnp.arange(N_DOM, dtype=jnp.int32)[:, None, None], send_blocks.shape)
    halo = blocks[:, owner, send_blocks]
    halo = jnp.transpose(halo, (0, 2, 1, 3, 4)).reshape(D, N_DOM, N_DOM * CAP, BLK)
    extended = jnp.concatenate([blocks, halo], axis=2)
    partition = jnp.arange(N_DOM, dtype=jnp.int32)[:, None]
    picked = extended[:, partition, tile_cols].astype(jnp.float32)
    live = (jnp.arange(TMAX, dtype=jnp.int32)[None, :] < tile_count[:, None]).astype(jnp.float32)
    values = tile_values.astype(jnp.float32) * live[:, :, None, None]
    rows_hot = jax.nn.one_hot(tile_rows, NBLK, dtype=jnp.float32)
    products = jnp.einsum('dptc,ptrc->dptr', picked, values, precision=highest)
    summed = jnp.einsum('dptr,ptb->dpbr', products, rows_hot, precision=highest)
    degree = jnp.einsum('ptr,ptb->pbr', lax.optimization_barrier(jnp.sum(values, axis=-1)), rows_hot, precision=highest)
    divisor = jnp.maximum(degree, 1.0)
    aggregate = (summed / divisor[None]).astype(jnp.bfloat16).reshape(D, NODES)
    pre_act = jnp.dot(weight_self.T, node_feats, preferred_element_type=jnp.float32)
    pre_act = pre_act + jnp.dot(weight_neigh.T, aggregate, preferred_element_type=jnp.float32)
    pre_act = pre_act + out_bias[:, None]
    layer_out = gelu_tanh(pre_act).astype(jnp.bfloat16)
    grad_pre = jax.vjp(gelu_tanh, pre_act)[1](out_cotangent.astype(jnp.float32))[0].astype(jnp.bfloat16)
    scale = 1.0 / jnp.sqrt(jnp.float32(NODES))
    grad_self = jnp.dot(node_feats, grad_pre.T, preferred_element_type=jnp.float32) * scale
    grad_neigh = jnp.dot(aggregate, grad_pre.T, preferred_element_type=jnp.float32) * scale
    grad_bias = lax.optimization_barrier(jnp.sum(grad_pre.astype(jnp.float32), axis=1)) * scale
    self_grad = jnp.dot(weight_self, grad_pre, preferred_element_type=jnp.float32)
    agg_grad = jnp.dot(weight_neigh, grad_pre, preferred_element_type=jnp.float32).reshape(D, N_DOM, NBLK, BLK)
    agg_grad = agg_grad / divisor[None]
    picked_grad = jnp.einsum('dpbr,ptb->dptr', agg_grad, rows_hot, precision=highest)
    contrib = jnp.einsum('dptr,ptrc->dptc', picked_grad, values, precision=highest)
    cols_hot = jax.nn.one_hot(tile_cols, NEXT, dtype=jnp.float32)
    ext_grad = jnp.einsum('dptc,ptn->dpnc', contrib, cols_hot, precision=highest)
    halo_grad = ext_grad[:, :, NBLK:].reshape(D, N_DOM, N_DOM, CAP, BLK)
    send_hot = jax.nn.one_hot(send_blocks, NBLK, dtype=jnp.float32)
    returned = jnp.einsum('dpqjc,qpjb->dqbc', halo_grad, send_hot, precision=highest)
    total = self_grad.reshape(D, N_DOM, NBLK, BLK) + ext_grad[:, :, :NBLK] + returned
    feats_grad = total.astype(jnp.bfloat16).reshape(D, NODES)
    return (layer_out, feats_grad, grad_self, grad_neigh, grad_bias)
```

```python
import jax
import jax.numpy as jnp
from jax import lax
from jax.experimental import pallas as pl
from jax.experimental.pallas import tpu as pltpu
from jax.sharding import PartitionSpec as P

BLK = 128
NBLK = 32
CAP = 2
TMAX = 64
ROWS = 4096
UNROLL = 8

SMEM = pl.BlockSpec(memory_space=pltpu.SMEM)
VMEM = pl.BlockSpec(memory_space=pltpu.VMEM)
PAIRS = [(i, i ^ 1) for i in range(32)]


def lanes(block):
    return pl.ds(pl.multiple_of(block * BLK, BLK), BLK)


def outgoing_kernel(sends, feats, out):
    for slot in range(out.shape[0] * CAP):
        part, place = divmod(slot, CAP)
        out[part, :, place * BLK : (place + 1) * BLK] = feats[:, lanes(sends[slot])]


def aggregate_kernel(rows, cols, count, feats, halo, tiles, out, divisor, ext, acc):
    width = feats.shape[0]
    ones = jnp.ones((16, BLK), jnp.bfloat16)
    for block in range(NBLK):
        ext[block, :width] = feats[:, block * BLK : (block + 1) * BLK]
        ext[block, width:] = ones
    for slot in range(halo.shape[0] * CAP):
        part, place = divmod(slot, CAP)
        ext[NBLK + slot, :width] = halo[part, :, place * BLK : (place + 1) * BLK]
        ext[NBLK + slot, width:] = ones
    acc[...] = jnp.zeros_like(acc)
    live = count[0]

    def step(group, carry):
        for inner in range(UNROLL):
            slot = group * UNROLL + inner
            alive = slot < live
            source = jnp.where(alive, cols[slot], 0)
            target = jnp.where(alive, rows[slot], NBLK)
            acc[target] += lax.dot_general(
                ext[source], tiles[slot], (((1,), (1,)), ((), ())), preferred_element_type=jnp.float32
            )
        return carry

    lax.fori_loop(0, (live + UNROLL - 1) // UNROLL, step, 0)
    for block in range(NBLK):
        chip, core = divmod(block, 2)
        span = slice(core * BLK, (core + 1) * BLK)
        div = jnp.maximum(acc[block, width : width + 1], 1.0)
        divisor[block : block + 1] = div
        out[2 * chip, :, span] = feats[:, block * BLK : (block + 1) * BLK]
        out[2 * chip + 1, :, span] = (acc[block, :width] / div).astype(jnp.bfloat16)


def scatter_kernel(rows, cols, count, back, divisor, tiles, halo, own, scaled, acc):
    width = own.shape[0]
    for block in range(NBLK):
        chip, core = divmod(block, 2)
        span = slice(core * BLK, (core + 1) * BLK)
        scaled[block] = (
            back[2 * chip + 1, :, span].astype(jnp.float32) / divisor[block : block + 1]
        ).astype(jnp.bfloat16)
        acc[block] = back[2 * chip, :, span].astype(jnp.float32)
    acc[NBLK:] = jnp.zeros((acc.shape[0] - NBLK, width, BLK), jnp.float32)
    live = count[0]
    spare = acc.shape[0] - 1

    def step(group, carry):
        for inner in range(UNROLL):
            slot = group * UNROLL + inner
            alive = slot < live
            source = jnp.where(alive, rows[slot], 0)
            target = jnp.where(alive, cols[slot], spare)
            acc[target] += jnp.dot(scaled[source], tiles[slot], preferred_element_type=jnp.float32)
        return carry

    lax.fori_loop(0, (live + UNROLL - 1) // UNROLL, step, 0)
    for block in range(NBLK):
        own[:, block * BLK : (block + 1) * BLK] = acc[block]
    for slot in range(halo.shape[0] * CAP):
        part, place = divmod(slot, CAP)
        halo[part, :, place * BLK : (place + 1) * BLK] = acc[NBLK + slot].astype(jnp.bfloat16)


def collect_kernel(sends, own, returned, out, acc):
    acc[...] = own[...]
    for slot in range(returned.shape[0] * CAP):
        part, place = divmod(slot, CAP)
        spot = lanes(sends[slot])
        acc[:, spot] += returned[part, :, place * BLK : (place + 1) * BLK].astype(jnp.float32)
    out[...] = acc[...].astype(jnp.bfloat16)


def pieces(values):
    high = lax.reduce_precision(values, 8, 7)
    rest = values - high
    middle = lax.reduce_precision(rest, 8, 7)
    low = rest - middle
    return jnp.stack([high, middle, low], axis=-1).astype(jnp.bfloat16)


def gelu_and_slope(v):
    root = 0.7978845608028654
    t = jnp.tanh(root * (v + 0.044715 * v * v * v))
    value = 0.5 * v * (1.0 + t)
    slope = 0.5 * (1.0 + t) + 0.5 * v * (1.0 - t * t) * (root * (1.0 + 3 * 0.044715 * v * v))
    return value, slope


def swap(values, axis):
    return lax.all_to_all(values, axis, split_axis=0, concat_axis=0, tiled=True)


def per_device(
    node_feats,
    out_cotangent,
    weight_self,
    weight_neigh,
    out_bias,
    send_blocks,
    tile_rows,
    tile_cols,
    tile_count,
    tile_values,
):
    f32, bf16 = jnp.float32, jnp.bfloat16
    width = node_feats.shape[0]
    parts = lax.axis_size("dom")
    shards = lax.axis_size("feat")
    dims = width * shards
    core = lax.axis_index("feat") % 2
    sends = send_blocks[0].reshape(parts * CAP)
    rows, cols, tiles = tile_rows[0], tile_cols[0], tile_values[0]

    outgoing = pl.pallas_call(
        outgoing_kernel,
        out_shape=jax.ShapeDtypeStruct((parts, width, CAP * BLK), bf16),
        in_specs=[SMEM, VMEM],
        out_specs=VMEM,
        name="outgoing",
    )(sends, node_feats)
    halo = swap(outgoing, "dom")

    both = jnp.stack([weight_self, weight_neigh])
    both = jnp.broadcast_to(both[None], (shards // 2, 2, width, dims)).reshape(shards, width, dims)
    cot = jnp.transpose(out_cotangent.reshape(width, NBLK, BLK), (1, 0, 2))
    bias = jnp.pad(pieces(out_bias), ((0, 0), (0, BLK - 3)))
    bias = jnp.broadcast_to(bias[None], (shards, width, BLK))
    packed = swap(jnp.concatenate([both, cot, bias], axis=2), "feat")
    packed = packed.reshape(dims, dims + 2 * BLK)
    weight = packed[:, :dims]
    cot = packed[:, dims : dims + BLK].astype(f32)
    bias = jnp.sum(packed[:, dims + BLK : dims + BLK + 3].astype(f32), axis=1, keepdims=True)

    spread, divisor = pl.pallas_call(
        aggregate_kernel,
        out_shape=(
            jax.ShapeDtypeStruct((shards, width, 2 * BLK), bf16),
            jax.ShapeDtypeStruct((NBLK, BLK), f32),
        ),
        in_specs=[SMEM, SMEM, SMEM, VMEM, VMEM, VMEM],
        out_specs=(VMEM, VMEM),
        scratch_shapes=[
            pltpu.VMEM((NBLK + parts * CAP, width + 16, BLK), bf16),
            pltpu.VMEM((NBLK + 1, width + 16, BLK), f32),
        ],
        name="aggregate",
    )(rows, cols, tile_count, node_feats, halo, tiles)
    data = swap(spread, "feat").reshape(dims, 2 * BLK)

    product = lax.dot_general(weight, data, (((0,), (0,)), ((), ())), preferred_element_type=f32)
    keep = lax.dynamic_slice(product, (0, core * BLK), (dims, BLK))
    send = lax.dynamic_slice(product, (0, (1 - core) * BLK), (dims, BLK))
    pre_act = keep + lax.ppermute(send, "feat", PAIRS) + bias
    value, slope = gelu_and_slope(pre_act)
    layer = value.astype(bf16)
    grad = (cot * slope).astype(bf16)
    other = lax.ppermute(grad, "feat", PAIRS)
    grads = jnp.where(
        core == 0, jnp.concatenate([grad, other], 1), jnp.concatenate([other, grad], 1)
    )
    back = jnp.dot(weight, grads, preferred_element_type=f32).astype(bf16)
    back = swap(back.reshape(shards, width, 2 * BLK), "feat")

    term = lax.dot_general(data, grads, (((1,), (1,)), ((), ())), preferred_element_type=f32)
    bias_sum = jnp.pad(pieces(jnp.sum(grad.astype(f32), axis=1)), ((0, 0), (0, BLK - 3)))
    joined = jnp.concatenate([term.astype(bf16), layer, bias_sum], axis=1)
    joined = swap(joined.reshape(shards, width, dims + 2 * BLK), "feat")
    layer_out = jnp.transpose(joined[:, :, dims : dims + BLK], (1, 0, 2)).reshape(width, ROWS)
    sums = jnp.sum(
        joined[:, :, :dims].reshape(shards // 2, 2, width, dims).astype(f32), axis=0
    )
    bias_part = jnp.sum(joined[:, :, dims + BLK : dims + BLK + 3].astype(f32), axis=(0, 2))

    halo_grad, own = pl.pallas_call(
        scatter_kernel,
        out_shape=(
            jax.ShapeDtypeStruct((parts, width, CAP * BLK), bf16),
            jax.ShapeDtypeStruct((width, ROWS), f32),
        ),
        in_specs=[SMEM, SMEM, SMEM, VMEM, VMEM, VMEM],
        out_specs=(VMEM, VMEM),
        scratch_shapes=[
            pltpu.VMEM((NBLK, width, BLK), bf16),
            pltpu.VMEM((NBLK + parts * CAP + 1, width, BLK), f32),
        ],
        name="scatter",
    )(rows, cols, tile_count, back, divisor, tiles)
    returned = swap(halo_grad, "dom")
    feats_grad = pl.pallas_call(
        collect_kernel,
        out_shape=jax.ShapeDtypeStruct((width, ROWS), bf16),
        in_specs=[SMEM, VMEM, VMEM],
        out_specs=VMEM,
        scratch_shapes=[pltpu.VMEM((width, ROWS), f32)],
        name="collect",
    )(sends, own, returned)

    chunk = 2 * dims // parts
    cut = jnp.transpose(sums.reshape(2, width, parts // 2, chunk), (0, 2, 1, 3))
    cut = cut.reshape(parts, width, chunk).astype(bf16)
    extra = jnp.pad(pieces(bias_part).T, ((0, 13), (0, BLK - width)))
    cut = jnp.concatenate([cut, jnp.broadcast_to(extra[None], (parts, 16, BLK))], axis=1)
    cut = swap(cut, "dom").astype(f32)
    scale = 1.0 / jnp.sqrt(f32(ROWS * parts))
    piece = jnp.sum(cut[:, :width], axis=0) * scale
    grad_bias = jnp.sum(cut[:, width : width + 3, :width], axis=(0, 1)) * scale
    whole = swap(jnp.broadcast_to(piece[None], (parts, width, chunk)), "dom")
    whole = jnp.transpose(whole.reshape(2, parts // 2, width, chunk), (0, 2, 1, 3))
    whole = whole.reshape(2, width, dims)
    return (layer_out, feats_grad, whole[0], whole[1], grad_bias)


def solution(mesh):
    in_specs = (
        P("feat", "dom"),
        P("feat", "dom"),
        P("feat", None),
        P("feat", None),
        P("feat"),
        P("dom", None, None),
        P("dom", None),
        P("dom", None),
        P("dom"),
        P("dom", None, None, None),
    )
    out_specs = (P("feat", "dom"), P("feat", "dom"), P("feat", None), P("feat", None), P("feat"))
    return jax.shard_map(
        per_device, mesh=mesh, in_specs=in_specs, out_specs=out_specs, check_vma=False
    )
```

```python
import functools

import jax
import jax.numpy as jnp
from jax import lax
from jax.experimental import pallas as pl
from jax.experimental.pallas import tpu as pltpu
from jax.sharding import PartitionSpec as P

BLK = 128
NBLK = 32
CAP = 2
TMAX = 64
ROWS = 4096
UNROLL = 8

SMEM = pl.BlockSpec(memory_space=pltpu.SMEM)
VMEM = pl.BlockSpec(memory_space=pltpu.VMEM)
PAIRS = [(i, i ^ 1) for i in range(32)]


def lanes(block):
    return pl.ds(pl.multiple_of(block * BLK, BLK), BLK)


def outgoing_kernel(sends, feats, out):
    for part in range(out.shape[0]):
        for place in range(CAP):
            out[part, :, place * BLK : (place + 1) * BLK] = feats[:, lanes(sends[0, part, place])]


def pack_kernel(weight_self, weight_neigh, cotangent, bias, out):
    own, neigh, extra = weight_self[...], weight_neigh[...], bias[...]
    dims = own.shape[1]
    for peer in range(out.shape[0]):
        out[peer, :, :dims] = own if peer % 2 == 0 else neigh
        out[peer, :, dims : dims + BLK] = cotangent[:, peer * BLK : (peer + 1) * BLK]
        out[peer, :, dims + BLK :] = extra


def aggregate_kernel(rows, cols, count, feats, halo, tiles, packed, out, divisor, ext, acc):
    width = feats.shape[0]
    ones = jnp.ones((16, BLK), jnp.bfloat16)
    for block in range(NBLK):
        ext[block, :width] = feats[:, block * BLK : (block + 1) * BLK]
        ext[block, width:] = ones
    for slot in range(halo.shape[0] * CAP):
        part, place = divmod(slot, CAP)
        ext[NBLK + slot, :width] = halo[part, :, place * BLK : (place + 1) * BLK]
        ext[NBLK + slot, width:] = ones
    acc[...] = jnp.zeros_like(acc)
    live = count[0]

    def step(group, carry):
        for inner in range(UNROLL):
            slot = group * UNROLL + inner
            alive = slot < live
            source = jnp.where(alive, cols[0, slot], 0)
            target = jnp.where(alive, rows[0, slot], NBLK)
            acc[target] += lax.dot_general(
                ext[source], tiles[slot], (((1,), (1,)), ((), ())), preferred_element_type=jnp.float32
            )
        return carry

    lax.fori_loop(0, (live + UNROLL - 1) // UNROLL, step, 0)
    for block in range(NBLK):
        chip, core = divmod(block, 2)
        span = slice(core * BLK, (core + 1) * BLK)
        div = jnp.maximum(acc[block, width : width + 1], 1.0)
        divisor[block : block + 1] = div
        out[2 * chip, :, span] = feats[:, block * BLK : (block + 1) * BLK]
        out[2 * chip + 1, :, span] = (acc[block, :width] / div).astype(jnp.bfloat16)


def pre_kernel(core, weight, data, keep, send):
    product = lax.dot_general(
        weight[...], data[...], (((0,), (0,)), ((), ())), preferred_element_type=jnp.float32
    )
    first, second = product[:, :BLK], product[:, BLK:]
    even = core[0] == 0
    keep[...] = jnp.where(even, first, second)
    send[...] = jnp.where(even, second, first)


def slope_kernel(keep, received, side, layer, grad, sums):
    cotangent = side[:, :BLK].astype(jnp.float32)
    bias = jnp.sum(side[:, BLK:].astype(jnp.float32), axis=1, keepdims=True)
    value, slope = gelu_and_slope(keep[...] + received[...] + bias)
    layer[...] = value.astype(jnp.bfloat16)
    rounded = (cotangent * slope).astype(jnp.bfloat16)
    grad[...] = rounded
    total = jnp.sum(rounded.astype(jnp.float32), axis=1, keepdims=True)
    high = total.astype(jnp.bfloat16).astype(jnp.float32)
    middle = (total - high).astype(jnp.bfloat16).astype(jnp.float32)
    low = total - high - middle
    lane = lax.broadcasted_iota(jnp.int32, (total.shape[0], BLK), 1)
    spread = jnp.where(lane == 0, high, jnp.where(lane == 1, middle, jnp.where(lane == 2, low, 0.0)))
    sums[...] = spread.astype(jnp.bfloat16)


def back_kernel(core, weight, data, grad, other, layer, sums, out, both):
    dims = weight.shape[1]

    @pl.when(pl.program_id(0) == 0)
    def _():
        even = core[0] == 0
        both[:, :BLK] = jnp.where(even, grad[...], other[...])
        both[:, BLK:] = jnp.where(even, other[...], grad[...])

    out[:, :dims] = lax.dot_general(
        data[...], both[...], (((1,), (1,)), ((), ())), preferred_element_type=jnp.float32
    ).astype(jnp.bfloat16)
    out[:, dims : dims + BLK] = layer[...]
    out[:, dims + BLK : dims + 2 * BLK] = sums[...]
    out[:, dims + 2 * BLK :] = jnp.dot(
        weight[...], both[...], preferred_element_type=jnp.float32
    ).astype(jnp.bfloat16)


def scatter_kernel(rows, cols, count, joined, divisor, tiles, out, own, scaled, acc):
    width = own.shape[0]
    start = joined.shape[2] - 2 * BLK
    for block in range(NBLK):
        chip, core = divmod(block, 2)
        span = slice(start + core * BLK, start + (core + 1) * BLK)
        scaled[block] = (
            joined[2 * chip + 1, :, span].astype(jnp.float32) / divisor[block : block + 1]
        ).astype(jnp.bfloat16)
        acc[block] = joined[2 * chip, :, span].astype(jnp.float32)
    acc[NBLK:] = jnp.zeros((acc.shape[0] - NBLK, width, BLK), jnp.float32)
    live = count[0]
    spare = acc.shape[0] - 1

    def step(group, carry):
        for inner in range(UNROLL):
            slot = group * UNROLL + inner
            alive = slot < live
            source = jnp.where(alive, rows[0, slot], 0)
            target = jnp.where(alive, cols[0, slot], spare)
            acc[target] += jnp.dot(scaled[source], tiles[slot], preferred_element_type=jnp.float32)
        return carry

    lax.fori_loop(0, (live + UNROLL - 1) // UNROLL, step, 0)
    for block in range(NBLK):
        own[:, block * BLK : (block + 1) * BLK] = acc[block]
    for slot in range(out.shape[0] * CAP):
        part, place = divmod(slot, CAP)
        out[part, :, place * BLK : (place + 1) * BLK] = acc[NBLK + slot].astype(jnp.bfloat16)
    for part in range(out.shape[0]):
        half, place = divmod(part, out.shape[0] // 2)
        span = slice(place * BLK, (place + 1) * BLK)
        total = joined[half, :, span].astype(jnp.float32)
        for chip in range(1, joined.shape[0] // 2):
            total += joined[2 * chip + half, :, span].astype(jnp.float32)
        out[part, :, CAP * BLK :] = total.astype(jnp.bfloat16)


def piece_kernel(terms, extra, out, *, scale):
    total = terms[0].astype(jnp.float32)
    for part in range(1, terms.shape[0]):
        total += terms[part].astype(jnp.float32)
    total = (total * scale).astype(jnp.bfloat16)
    for part in range(out.shape[0]):
        out[part, : total.shape[0]] = total
        out[part, total.shape[0] :] = extra[...]


def collect_kernel(sends, own, returned, out, acc):
    acc[...] = own[...]
    for part in range(returned.shape[0]):
        for place in range(CAP):
            spot = lanes(sends[0, part, place])
            acc[:, spot] += returned[part, :, place * BLK : (place + 1) * BLK].astype(jnp.float32)
    out[...] = acc[...].astype(jnp.bfloat16)


def finish_kernel(chunks, grad_self, grad_neigh):
    width = grad_self.shape[0]
    count = chunks.shape[0] // 2
    for place in range(count):
        span = slice(place * BLK, (place + 1) * BLK)
        grad_self[:, span] = chunks[place, :width].astype(jnp.float32)
        grad_neigh[:, span] = chunks[count + place, :width].astype(jnp.float32)


def whole(*shape):
    return pl.BlockSpec(shape, lambda *_: (0,) * len(shape))


def part_of(shape, *index):
    return pl.BlockSpec(shape, lambda *_: index)


def pieces(values):
    high = lax.reduce_precision(values, 8, 7)
    rest = values - high
    middle = lax.reduce_precision(rest, 8, 7)
    low = rest - middle
    return jnp.stack([high, middle, low], axis=-1).astype(jnp.bfloat16)


def gelu_and_slope(v):
    root = 0.7978845608028654
    t = jnp.tanh(root * (v + 0.044715 * v * v * v))
    value = 0.5 * v * (1.0 + t)
    slope = 0.5 * (1.0 + t) + 0.5 * v * (1.0 - t * t) * (root * (1.0 + 3 * 0.044715 * v * v))
    return value, slope


def swap(values, axis):
    return lax.all_to_all(values, axis, split_axis=0, concat_axis=0, tiled=True)


def per_device(
    node_feats,
    out_cotangent,
    weight_self,
    weight_neigh,
    out_bias,
    send_blocks,
    tile_rows,
    tile_cols,
    tile_count,
    tile_values,
):
    f32, bf16 = jnp.float32, jnp.bfloat16
    width = node_feats.shape[0]
    parts = lax.axis_size("dom")
    shards = lax.axis_size("feat")
    dims = width * shards
    total = dims + 4 * BLK
    core = (lax.axis_index("feat") % 2).astype(jnp.int32).reshape(1)
    tiles = tile_values[0]

    outgoing = pl.pallas_call(
        outgoing_kernel,
        out_shape=jax.ShapeDtypeStruct((parts, width, CAP * BLK), bf16),
        in_specs=[SMEM, VMEM],
        out_specs=VMEM,
        name="outgoing",
    )(send_blocks, node_feats)
    halo = swap(outgoing, "dom")

    bias = jnp.pad(pieces(out_bias), ((0, 0), (0, BLK - 3)))
    packed = pl.pallas_call(
        pack_kernel,
        out_shape=jax.ShapeDtypeStruct((shards, width, total), bf16),
        grid=(1,),
        in_specs=[whole(width, dims), whole(width, dims), whole(width, ROWS), whole(width, BLK)],
        out_specs=part_of((shards, width, dims + 2 * BLK), 0, 0, 0),
        name="pack",
    )(weight_self, weight_neigh, out_cotangent, bias)

    packed, divisor = pl.pallas_call(
        aggregate_kernel,
        out_shape=(
            jax.ShapeDtypeStruct((shards, width, total), bf16),
            jax.ShapeDtypeStruct((NBLK, BLK), f32),
        ),
        grid=(1,),
        in_specs=[
            SMEM,
            SMEM,
            SMEM,
            whole(width, ROWS),
            whole(parts, width, CAP * BLK),
            whole(TMAX, BLK, BLK),
            pl.BlockSpec(memory_space=pl.ANY),
        ],
        out_specs=(part_of((shards, width, 2 * BLK), 0, 0, dims // (2 * BLK) + 1), whole(NBLK, BLK)),
        scratch_shapes=[
            pltpu.VMEM((NBLK + parts * CAP, width + 16, BLK), bf16),
            pltpu.VMEM((NBLK + 1, width + 16, BLK), f32),
        ],
        input_output_aliases={6: 0},
        name="aggregate",
    )(tile_rows, tile_cols, tile_count, node_feats, halo, tiles, packed)
    packed = swap(packed, "feat").reshape(dims, total)

    chunk = 2 * BLK
    last = dims // chunk + 1
    keep, send = pl.pallas_call(
        pre_kernel,
        out_shape=(jax.ShapeDtypeStruct((dims, BLK), f32),) * 2,
        grid=(dims // chunk,),
        in_specs=[
            SMEM,
            pl.BlockSpec((dims, chunk), lambda i: (0, i)),
            part_of((dims, chunk), 0, last),
        ],
        out_specs=(pl.BlockSpec((chunk, BLK), lambda i: (i, 0)),) * 2,
        name="pre",
    )(core, packed, packed)
    received = lax.ppermute(send, "feat", PAIRS)
    layer, grad, sums = pl.pallas_call(
        slope_kernel,
        out_shape=(jax.ShapeDtypeStruct((dims, BLK), bf16),) * 3,
        grid=(1,),
        in_specs=[whole(dims, BLK), whole(dims, BLK), part_of((dims, chunk), 0, last - 1)],
        out_specs=(whole(dims, BLK),) * 3,
        name="slope",
    )(keep, received, packed)
    other = lax.ppermute(grad, "feat", PAIRS)
    joined = pl.pallas_call(
        back_kernel,
        out_shape=jax.ShapeDtypeStruct((dims, total), bf16),
        grid=(dims // chunk,),
        in_specs=[
            SMEM,
            pl.BlockSpec((chunk, dims), lambda i: (i, 0)),
            pl.BlockSpec((chunk, chunk), lambda i: (i, last)),
            whole(dims, BLK),
            whole(dims, BLK),
            pl.BlockSpec((chunk, BLK), lambda i: (i, 0)),
            pl.BlockSpec((chunk, BLK), lambda i: (i, 0)),
        ],
        out_specs=pl.BlockSpec((chunk, total), lambda i: (i, 0)),
        scratch_shapes=[pltpu.VMEM((dims, chunk), bf16)],
        name="back",
    )(core, packed, packed, grad, other, layer, sums)
    joined = swap(joined.reshape(shards, width, total), "feat")

    outgoing, own = pl.pallas_call(
        scatter_kernel,
        out_shape=(
            jax.ShapeDtypeStruct((parts, width, (CAP + 1) * BLK), bf16),
            jax.ShapeDtypeStruct((width, ROWS), f32),
        ),
        grid=(1,),
        in_specs=[
            SMEM,
            SMEM,
            SMEM,
            whole(shards, width, total),
            whole(NBLK, BLK),
            whole(TMAX, BLK, BLK),
        ],
        out_specs=(whole(parts, width, (CAP + 1) * BLK), whole(width, ROWS)),
        scratch_shapes=[
            pltpu.VMEM((NBLK, width, BLK), bf16),
            pltpu.VMEM((NBLK + parts * CAP + 1, width, BLK), f32),
        ],
        name="scatter",
    )(tile_rows, tile_cols, tile_count, joined, divisor, tiles)
    returned = swap(outgoing, "dom")

    layer_out = jnp.transpose(joined[:, :, dims : dims + BLK], (1, 0, 2)).reshape(width, ROWS)
    bias_part = jnp.sum(joined[:, :, dims + BLK : dims + BLK + 3].astype(f32), axis=(0, 2))
    scale = 1.0 / float(ROWS * parts) ** 0.5
    extra = jnp.pad(pieces(bias_part * scale).T, ((0, 13), (0, BLK - width)))
    chunks = pl.pallas_call(
        functools.partial(piece_kernel, scale=scale),
        out_shape=jax.ShapeDtypeStruct((parts, width + 16, BLK), bf16),
        grid=(1,),
        in_specs=[part_of((parts, width, BLK), 0, 0, CAP), whole(16, BLK)],
        out_specs=whole(parts, width + 16, BLK),
        name="piece",
    )(returned, extra)
    chunks = swap(chunks, "dom")
    feats_grad = pl.pallas_call(
        collect_kernel,
        out_shape=jax.ShapeDtypeStruct((width, ROWS), bf16),
        grid=(1,),
        in_specs=[SMEM, whole(width, ROWS), part_of((parts, width, CAP * BLK), 0, 0, 0)],
        out_specs=whole(width, ROWS),
        scratch_shapes=[pltpu.VMEM((width, ROWS), f32)],
        name="collect",
    )(send_blocks, own, returned)
    grad_self, grad_neigh = pl.pallas_call(
        finish_kernel,
        out_shape=(jax.ShapeDtypeStruct((width, dims), f32),) * 2,
        in_specs=[VMEM],
        out_specs=(VMEM, VMEM),
        name="finish",
    )(chunks)
    grad_bias = jnp.sum(chunks[:, width : width + 3, :width].astype(f32), axis=(0, 1))
    return (layer_out, feats_grad, grad_self, grad_neigh, grad_bias)


def solution(mesh):
    in_specs = (
        P("feat", "dom"),
        P("feat", "dom"),
        P("feat", None),
        P("feat", None),
        P("feat"),
        P("dom", None, None),
        P("dom", None),
        P("dom", None),
        P("dom"),
        P("dom", None, None, None),
    )
    out_specs = (P("feat", "dom"), P("feat", "dom"), P("feat", None), P("feat", None), P("feat"))
    return jax.shard_map(
        per_device, mesh=mesh, in_specs=in_specs, out_specs=out_specs, check_vma=False
    )
```

```python
import functools

import jax
import jax.numpy as jnp
from jax import lax
from jax.experimental import pallas as pl
from jax.experimental.pallas import tpu as pltpu
from jax.sharding import PartitionSpec as P

BLK = 128
NBLK = 32
CAP = 2
TMAX = 64
ROWS = 4096
UNROLL = 8

SMEM = pl.BlockSpec(memory_space=pltpu.SMEM)
HBM = pltpu.MemorySpace.HBM
VMEM = pl.BlockSpec(memory_space=pltpu.VMEM)
PARAMS = pltpu.CompilerParams(vmem_limit_bytes=32 << 20)
PAIRS = [(i, i ^ 1) for i in range(32)]


def lanes(block):
    return pl.ds(pl.multiple_of(block * BLK, BLK), BLK)


def outgoing_kernel(sends, feats, out):
    for part in range(out.shape[0]):
        for place in range(CAP):
            out[part, :, place * BLK : (place + 1) * BLK] = feats[:, lanes(sends[0, place, part])]


def pack_kernel(weight_self, weight_neigh, cotangent, bias, out):
    own, neigh, extra = weight_self[...], weight_neigh[...], bias[...]
    dims = own.shape[1]
    for peer in range(out.shape[0]):
        out[peer, :, :dims] = own if peer % 2 == 0 else neigh
        out[peer, :, dims : dims + BLK] = cotangent[:, peer * BLK : (peer + 1) * BLK]
        out[peer, :, dims + BLK :] = extra


def aggregate_kernel(rows, cols, count, feats, halo, tiles, packed, out, divisor, ext, acc):
    width = feats.shape[0]
    ones = jnp.ones((16, BLK), jnp.bfloat16)
    for block in range(NBLK):
        ext[block, :width] = feats[:, block * BLK : (block + 1) * BLK]
        ext[block, width:] = ones
    for slot in range(halo.shape[0] * CAP):
        part, place = divmod(slot, CAP)
        ext[NBLK + slot, :width] = halo[part, :, place * BLK : (place + 1) * BLK]
        ext[NBLK + slot, width:] = ones
    acc[...] = jnp.zeros_like(acc)
    live = count[0]

    def step(group, carry):
        for inner in range(UNROLL):
            slot = group * UNROLL + inner
            alive = slot < live
            source = jnp.where(alive, cols[0, slot], 0)
            target = jnp.where(alive, rows[0, slot], NBLK)
            acc[target] += lax.dot_general(
                ext[source], tiles[slot], (((1,), (1,)), ((), ())), preferred_element_type=jnp.float32
            )
        return carry

    lax.fori_loop(0, (live + UNROLL - 1) // UNROLL, step, 0)
    for block in range(NBLK):
        chip, core = divmod(block, 2)
        span = slice(core * BLK, (core + 1) * BLK)
        div = jnp.maximum(acc[block, width : width + 1], 1.0)
        divisor[block : block + 1] = div
        out[2 * chip, :, span] = feats[:, block * BLK : (block + 1) * BLK]
        out[2 * chip + 1, :, span] = (acc[block, :width] / div).astype(jnp.bfloat16)


def pre_kernel(core, packed, keep, send):
    dims, chunk = keep.shape[0], 2 * BLK
    data = packed[:, dims + chunk :]
    even = core[0] == 0
    for start in range(0, dims, chunk):
        product = lax.dot_general(
            packed[:, start : start + chunk],
            data,
            (((0,), (0,)), ((), ())),
            preferred_element_type=jnp.float32,
        )
        first, second = product[:, :BLK], product[:, BLK:]
        keep[start : start + chunk] = jnp.where(even, first, second)
        send[start : start + chunk] = jnp.where(even, second, first)


def slope_kernel(keep, received, packed, layer, grad, local, sums):
    dims = keep.shape[0]
    cotangent = packed[:, dims : dims + BLK].astype(jnp.float32)
    bias = packed[:, dims + BLK : dims + 2 * BLK].astype(jnp.float32)
    bias = jnp.sum(bias, axis=1, keepdims=True)
    value, slope = gelu_and_slope(keep[...] + received[...] + bias)
    layer[...] = value.astype(jnp.bfloat16)
    rounded = (cotangent * slope).astype(jnp.bfloat16)
    grad[...] = rounded
    local[...] = rounded
    total = jnp.sum(rounded.astype(jnp.float32), axis=1, keepdims=True)
    high = total.astype(jnp.bfloat16).astype(jnp.float32)
    middle = (total - high).astype(jnp.bfloat16).astype(jnp.float32)
    low = total - high - middle
    lane = lax.broadcasted_iota(jnp.int32, (total.shape[0], BLK), 1)
    spread = jnp.where(lane == 0, high, jnp.where(lane == 1, middle, jnp.where(lane == 2, low, 0.0)))
    sums[...] = spread.astype(jnp.bfloat16)


def back_kernel(core, packed, grad, other, layer, sums, out, both):
    rows, total = out.shape
    dims = total - 4 * BLK
    span = pl.ds(pl.multiple_of(pl.program_id(0) * rows, rows), rows)

    @pl.when(pl.program_id(0) == 0)
    def _():
        even = core[0] == 0
        both[:, :BLK] = jnp.where(even, grad[...], other[...])
        both[:, BLK:] = jnp.where(even, other[...], grad[...])

    out[:, :dims] = lax.dot_general(
        packed[span, dims + 2 * BLK :],
        both[...],
        (((1,), (1,)), ((), ())),
        preferred_element_type=jnp.float32,
    ).astype(jnp.bfloat16)
    out[:, dims : dims + BLK] = layer[span]
    out[:, dims + BLK : dims + 2 * BLK] = sums[span]
    out[:, dims + 2 * BLK :] = jnp.dot(
        packed[span, :dims], both[...], preferred_element_type=jnp.float32
    ).astype(jnp.bfloat16)


def scatter_kernel(rows, cols, count, joined, divisor, tiles, out, own, scaled, acc):
    width = own.shape[0]
    start = joined.shape[2] - 2 * BLK
    for block in range(NBLK):
        chip, core = divmod(block, 2)
        span = slice(start + core * BLK, start + (core + 1) * BLK)
        scaled[block] = (
            joined[2 * chip + 1, :, span].astype(jnp.float32) / divisor[block : block + 1]
        ).astype(jnp.bfloat16)
        acc[block] = joined[2 * chip, :, span].astype(jnp.float32)
    acc[NBLK:] = jnp.zeros((acc.shape[0] - NBLK, width, BLK), jnp.float32)
    live = count[0]
    spare = acc.shape[0] - 1

    def step(group, carry):
        for inner in range(UNROLL):
            slot = group * UNROLL + inner
            alive = slot < live
            source = jnp.where(alive, rows[0, slot], 0)
            target = jnp.where(alive, cols[0, slot], spare)
            acc[target] += jnp.dot(scaled[source], tiles[slot], preferred_element_type=jnp.float32)
        return carry

    lax.fori_loop(0, (live + UNROLL - 1) // UNROLL, step, 0)
    for block in range(NBLK):
        own[:, block * BLK : (block + 1) * BLK] = acc[block]
    for slot in range(out.shape[0] * CAP):
        part, place = divmod(slot, CAP)
        out[part, :, place * BLK : (place + 1) * BLK] = acc[NBLK + slot].astype(jnp.bfloat16)
    for part in range(out.shape[0]):
        half, place = divmod(part, out.shape[0] // 2)
        span = slice(place * BLK, (place + 1) * BLK)
        total = joined[half, :, span].astype(jnp.float32)
        for chip in range(1, joined.shape[0] // 2):
            total += joined[2 * chip + half, :, span].astype(jnp.float32)
        out[part, :, CAP * BLK :] = total.astype(jnp.bfloat16)


def piece_kernel(terms, extra, out, *, scale):
    total = terms[0, :, CAP * BLK :].astype(jnp.float32)
    for part in range(1, terms.shape[0]):
        total += terms[part, :, CAP * BLK :].astype(jnp.float32)
    total = (total * scale).astype(jnp.bfloat16)
    for part in range(out.shape[0]):
        out[part, : total.shape[0]] = total
        out[part, total.shape[0] :] = extra[...]


def collect_kernel(sends, own, returned, out, acc):
    acc[...] = own[...]
    for part in range(returned.shape[0]):
        for place in range(CAP):
            spot = lanes(sends[0, place, part])
            acc[:, spot] += returned[part, :, place * BLK : (place + 1) * BLK].astype(jnp.float32)
    out[...] = acc[...].astype(jnp.bfloat16)


def finish_kernel(chunks, grad_self, grad_neigh):
    width = grad_self.shape[0]
    count = chunks.shape[0] // 2
    for place in range(count):
        span = slice(place * BLK, (place + 1) * BLK)
        grad_self[:, span] = chunks[place, :width].astype(jnp.float32)
        grad_neigh[:, span] = chunks[count + place, :width].astype(jnp.float32)


def whole(*shape):
    return pl.BlockSpec(shape, lambda *_: (0,) * len(shape))


def near(array):
    return pltpu.with_memory_space_constraint(array, pltpu.MemorySpace.VMEM)


def part_of(shape, *index):
    return pl.BlockSpec(shape, lambda *_: index)


def pieces(values):
    high = lax.reduce_precision(values, 8, 7)
    rest = values - high
    middle = lax.reduce_precision(rest, 8, 7)
    low = rest - middle
    return jnp.stack([high, middle, low], axis=-1).astype(jnp.bfloat16)


def gelu_and_slope(v):
    root = 0.7978845608028654
    t = jnp.tanh(root * (v + 0.044715 * v * v * v))
    value = 0.5 * v * (1.0 + t)
    slope = 0.5 * (1.0 + t) + 0.5 * v * (1.0 - t * t) * (root * (1.0 + 3 * 0.044715 * v * v))
    return value, slope


def swap(values, axis):
    return lax.all_to_all(values, axis, split_axis=0, concat_axis=0, tiled=True)


def per_device(
    node_feats,
    out_cotangent,
    weight_self,
    weight_neigh,
    out_bias,
    send_blocks,
    tile_rows,
    tile_cols,
    tile_count,
    tile_values,
):
    f32, bf16 = jnp.float32, jnp.bfloat16
    width = node_feats.shape[0]
    parts = lax.axis_size("dom")
    shards = lax.axis_size("feat")
    dims = width * shards
    total = dims + 4 * BLK
    send_blocks = jnp.transpose(send_blocks, (0, 2, 1))
    core = (lax.axis_index("feat") % 2).astype(jnp.int32).reshape(1)
    tiles = near(tile_values[0])

    outgoing = pl.pallas_call(
        outgoing_kernel,
        out_shape=jax.ShapeDtypeStruct((parts, width, CAP * BLK), bf16),
        in_specs=[SMEM, VMEM],
        out_specs=VMEM,
        compiler_params=PARAMS,
        name="outgoing",
    )(send_blocks, node_feats)
    halo = swap(outgoing, "dom")

    bias = jnp.pad(pieces(out_bias), ((0, 0), (0, BLK - 3)))
    packed = pl.pallas_call(
        pack_kernel,
        out_shape=HBM((shards, width, total), bf16),
        grid=(1,),
        in_specs=[whole(width, dims), whole(width, dims), whole(width, ROWS), whole(width, BLK)],
        out_specs=part_of((shards, width, dims + 2 * BLK), 0, 0, 0),
        compiler_params=PARAMS,
        name="pack",
    )(weight_self, weight_neigh, out_cotangent, bias)

    packed, divisor = pl.pallas_call(
        aggregate_kernel,
        out_shape=(
            HBM((shards, width, total), bf16),
            pltpu.VMEM((NBLK, BLK), f32),
        ),
        grid=(1,),
        in_specs=[
            SMEM,
            SMEM,
            SMEM,
            VMEM,
            VMEM,
            VMEM,
            pl.BlockSpec(memory_space=pl.ANY),
        ],
        out_specs=(part_of((shards, width, 2 * BLK), 0, 0, dims // (2 * BLK) + 1), VMEM),
        scratch_shapes=[
            pltpu.VMEM((NBLK + parts * CAP, width + 16, BLK), bf16),
            pltpu.VMEM((NBLK + 1, width + 16, BLK), f32),
        ],
        input_output_aliases={6: 0},
        compiler_params=PARAMS,
        name="aggregate",
    )(tile_rows, tile_cols, tile_count, near(node_feats), near(halo), tiles, packed)
    packed = near(swap(packed, "feat").reshape(dims, total))

    chunk = 2 * BLK
    keep, send = pl.pallas_call(
        pre_kernel,
        out_shape=(pltpu.VMEM((dims, BLK), f32), jax.ShapeDtypeStruct((dims, BLK), f32)),
        in_specs=[SMEM, VMEM],
        out_specs=(VMEM, VMEM),
        compiler_params=PARAMS,
        name="pre",
    )(core, packed)
    received = lax.ppermute(send, "feat", PAIRS)
    layer, grad, local, sums = pl.pallas_call(
        slope_kernel,
        out_shape=(
            pltpu.VMEM((dims, BLK), bf16),
            jax.ShapeDtypeStruct((dims, BLK), bf16),
            pltpu.VMEM((dims, BLK), bf16),
            pltpu.VMEM((dims, BLK), bf16),
        ),
        in_specs=[VMEM, VMEM, VMEM],
        out_specs=(VMEM,) * 4,
        compiler_params=PARAMS,
        name="slope",
    )(near(keep), near(received), packed)
    other = lax.ppermute(grad, "feat", PAIRS)
    joined = pl.pallas_call(
        back_kernel,
        out_shape=jax.ShapeDtypeStruct((dims, total), bf16),
        grid=(dims // chunk,),
        in_specs=[SMEM, VMEM, VMEM, VMEM, VMEM, VMEM],
        out_specs=pl.BlockSpec((chunk, total), lambda i: (i, 0)),
        scratch_shapes=[pltpu.VMEM((dims, chunk), bf16)],
        compiler_params=PARAMS,
        name="back",
    )(core, packed, near(local), near(other), near(layer), near(sums))
    joined = swap(joined.reshape(shards, width, total), "feat")

    outgoing, own = pl.pallas_call(
        scatter_kernel,
        out_shape=(
            HBM((parts, width, (CAP + 1) * BLK), bf16),
            pltpu.VMEM((width, ROWS), f32),
        ),
        in_specs=[SMEM, SMEM, SMEM, VMEM, VMEM, VMEM],
        out_specs=(VMEM, VMEM),
        scratch_shapes=[
            pltpu.VMEM((NBLK, width, BLK), bf16),
            pltpu.VMEM((NBLK + parts * CAP + 1, width, BLK), f32),
        ],
        compiler_params=PARAMS,
        name="scatter",
    )(tile_rows, tile_cols, tile_count, near(joined), near(divisor), tiles)
    returned = near(swap(outgoing, "dom"))

    layer_out = jnp.transpose(joined[:, :, dims : dims + BLK], (1, 0, 2)).reshape(width, ROWS)
    bias_part = jnp.sum(joined[:, :, dims + BLK : dims + BLK + 3].astype(f32), axis=(0, 2))
    scale = 1.0 / float(ROWS * parts) ** 0.5
    extra = jnp.pad(pieces(bias_part * scale).T, ((0, 13), (0, BLK - width)))
    chunks = pl.pallas_call(
        functools.partial(piece_kernel, scale=scale),
        out_shape=HBM((parts, width + 16, BLK), bf16),
        in_specs=[VMEM, VMEM],
        out_specs=VMEM,
        compiler_params=PARAMS,
        name="piece",
    )(returned, near(extra))
    chunks = swap(chunks, "dom")
    feats_grad = pl.pallas_call(
        collect_kernel,
        out_shape=jax.ShapeDtypeStruct((width, ROWS), bf16),
        in_specs=[SMEM, VMEM, VMEM],
        out_specs=VMEM,
        scratch_shapes=[pltpu.VMEM((width, ROWS), f32)],
        compiler_params=PARAMS,
        name="collect",
    )(send_blocks, near(own), returned)
    grad_self, grad_neigh = pl.pallas_call(
        finish_kernel,
        out_shape=(jax.ShapeDtypeStruct((width, dims), f32),) * 2,
        in_specs=[VMEM],
        out_specs=(VMEM, VMEM),
        compiler_params=PARAMS,
        name="finish",
    )(near(chunks))
    grad_bias = jnp.sum(chunks[:, width : width + 3, :width].astype(f32), axis=(0, 1))
    return (layer_out, feats_grad, grad_self, grad_neigh, grad_bias)


def solution(mesh):
    in_specs = (
        P("feat", "dom"),
        P("feat", "dom"),
        P("feat", None),
        P("feat", None),
        P("feat"),
        P("dom", None, None),
        P("dom", None),
        P("dom", None),
        P("dom"),
        P("dom", None, None, None),
    )
    out_specs = (P("feat", "dom"), P("feat", "dom"), P("feat", None), P("feat", None), P("feat"))
    return jax.shard_map(
        per_device, mesh=mesh, in_specs=in_specs, out_specs=out_specs, check_vma=False
    )
```

```python
import functools

import jax
import jax.numpy as jnp
from jax import lax
from jax.experimental import pallas as pl
from jax.experimental.pallas import tpu as pltpu
from jax.sharding import PartitionSpec as P

BLK = 128
NBLK = 32
CAP = 2
TMAX = 64
ROWS = 4096
UNROLL = 8

SMEM = pl.BlockSpec(memory_space=pltpu.SMEM)
HBM = pltpu.MemorySpace.HBM
VMEM = pl.BlockSpec(memory_space=pltpu.VMEM)
PARAMS = pltpu.CompilerParams(vmem_limit_bytes=32 << 20)
PAIRS = [(i, i ^ 1) for i in range(32)]


def lanes(block):
    return pl.ds(pl.multiple_of(block * BLK, BLK), BLK)


def outgoing_kernel(sends, feats, out):
    for part in range(out.shape[0]):
        for place in range(CAP):
            out[part, :, place * BLK : (place + 1) * BLK] = feats[:, lanes(sends[0, place, part])]


SIDE = 8 * 32
TAIL = 9 * 32
HEIGHT = TAIL + 16


def interleave():
    lane = lax.broadcasted_iota(jnp.int32, (2 * BLK, 2 * BLK), 0)
    spot = lax.broadcasted_iota(jnp.int32, (2 * BLK, 2 * BLK), 1)
    goal = (lane % 32) // 16 * BLK + lane // 32 * 16 + lane % 16
    return jnp.where(goal == spot, 1.0, 0.0).astype(jnp.bfloat16)


def pack_kernel(weight_self, weight_neigh, cotangent, bias, out):
    order = interleave()
    for path, weight in enumerate((weight_self, weight_neigh)):
        for block in range(weight.shape[1] // (2 * BLK)):
            mixed = jnp.dot(
                weight[:, 2 * block * BLK : 2 * (block + 1) * BLK],
                order,
                preferred_element_type=jnp.float32,
            ).astype(jnp.bfloat16)
            for half in range(2):
                part = mixed[:, half * BLK : (half + 1) * BLK]
                for group in range(out.shape[0] // 4):
                    out[4 * group + 2 * half + path, block * 32 : (block + 1) * 32] = part
    for peer in range(out.shape[0]):
        half = peer // 2 % 2
        first = 4 * (peer // 4) + 2 * (peer % 2)
        rows = slice(half * 16, (half + 1) * 16)
        for place in range(2):
            out[peer, SIDE + 16 * place : SIDE + 16 * (place + 1)] = cotangent[
                rows, (first + place) * BLK : (first + place + 1) * BLK
            ]
        out[peer, TAIL:] = bias[rows]


def aggregate_kernel(rows, cols, count, feats, halo, tiles, packed, out, divisor, ext, acc):
    width = feats.shape[0]
    ones = jnp.ones((16, BLK), jnp.bfloat16)
    for block in range(NBLK):
        ext[block, :width] = feats[:, block * BLK : (block + 1) * BLK]
        ext[block, width:] = ones
    for slot in range(halo.shape[0] * CAP):
        part, place = divmod(slot, CAP)
        ext[NBLK + slot, :width] = halo[part, :, place * BLK : (place + 1) * BLK]
        ext[NBLK + slot, width:] = ones
    acc[...] = jnp.zeros_like(acc)
    live = count[0]

    def step(group, carry):
        for inner in range(UNROLL):
            slot = group * UNROLL + inner
            alive = slot < live
            source = jnp.where(alive, cols[0, slot], 0)
            target = jnp.where(alive, rows[0, slot], NBLK)
            acc[target] += lax.dot_general(
                ext[source], tiles[slot], (((1,), (1,)), ((), ())), preferred_element_type=jnp.float32
            )
        return carry

    lax.fori_loop(0, (live + UNROLL - 1) // UNROLL, step, 0)
    for block in range(NBLK):
        group, place = divmod(block, 4)
        span = slice(place * 32, (place + 1) * 32)
        div = jnp.maximum(acc[block, width : width + 1], 1.0)
        divisor[block : block + 1] = div
        mean = (acc[block, :width] / div).astype(jnp.bfloat16)
        for half in range(2):
            out[4 * group + 2 * half, span] = feats[:, block * BLK : (block + 1) * BLK]
            out[4 * group + 2 * half + 1, span] = mean


def pre_kernel(core, packed, weight, data, keep, send):
    dims, outs = weight.shape
    for block in range(4):
        span = slice(block * BLK, (block + 1) * BLK)
        weight[:, span] = packed[:, block * 32 : (block + 1) * 32].reshape(dims, BLK)
        data[:, span] = packed[:, (4 + block) * 32 : (5 + block) * 32].reshape(dims, BLK)
    even = core[0] == 0
    for start in range(0, outs, 2 * BLK):
        rows = slice(start, start + 2 * BLK)
        product = lax.dot_general(
            weight[:, rows], data[...], (((0,), (0,)), ((), ())), preferred_element_type=jnp.float32
        )
        first, second = product[:, : 2 * BLK], product[:, 2 * BLK :]
        keep[rows] = jnp.where(even, first, second)
        send[rows] = jnp.where(even, second, first)


def slope_kernel(keep, received, packed, layer, grad, local, sums):
    outs = keep.shape[0]
    bias = packed[:, TAIL:].reshape(outs, BLK).astype(jnp.float32)
    bias = jnp.sum(bias, axis=1, keepdims=True)
    total = jnp.zeros((outs, 1), jnp.float32)
    for place in range(2):
        span = slice(place * BLK, (place + 1) * BLK)
        cotangent = packed[:, SIDE + 16 * place : SIDE + 16 * (place + 1)].reshape(outs, BLK)
        value, slope = gelu_and_slope(keep[:, span] + received[:, span] + bias)
        layer[:, span] = value.astype(jnp.bfloat16)
        rounded = (cotangent.astype(jnp.float32) * slope).astype(jnp.bfloat16)
        grad[:, span] = rounded
        local[:, span] = rounded
        total += jnp.sum(rounded.astype(jnp.float32), axis=1, keepdims=True)
    high = total.astype(jnp.bfloat16).astype(jnp.float32)
    middle = (total - high).astype(jnp.bfloat16).astype(jnp.float32)
    low = total - high - middle
    lane = lax.broadcasted_iota(jnp.int32, (outs, BLK), 1)
    spread = jnp.where(lane == 0, high, jnp.where(lane == 1, middle, jnp.where(lane == 2, low, 0.0)))
    sums[...] = spread.astype(jnp.bfloat16)


def back_kernel(core, weight, data, grad, other, layer, sums, out, both):
    peers = out.shape[0]
    rows = pl.ds(pl.multiple_of(pl.program_id(0) * peers * 32, peers * 32), peers * 32)
    outs = pl.ds(pl.multiple_of(pl.program_id(0) * peers * 16, peers * 16), peers * 16)

    @pl.when(pl.program_id(0) == 0)
    def _():
        even = core[0] == 0
        both[:, : 2 * BLK] = jnp.where(even, grad[...], other[...])
        both[:, 2 * BLK :] = jnp.where(even, other[...], grad[...])

    term = lax.dot_general(
        data[rows], both[...], (((1,), (1,)), ((), ())), preferred_element_type=jnp.float32
    ).astype(jnp.bfloat16)
    back = jnp.dot(weight[rows], both[...], preferred_element_type=jnp.float32).astype(jnp.bfloat16)
    for block in range(4):
        span = slice(block * BLK, (block + 1) * BLK)
        out[:, block * 32 : (block + 1) * 32] = term[:, span].reshape(peers, 32, BLK)
        out[:, (4 + block) * 32 : (5 + block) * 32] = back[:, span].reshape(peers, 32, BLK)
    for place in range(2):
        value = layer[outs, place * BLK : (place + 1) * BLK]
        out[:, SIDE + 16 * place : SIDE + 16 * (place + 1)] = value.reshape(peers, 16, BLK)
    out[:, TAIL:] = sums[outs].reshape(peers, 16, BLK)


def scatter_kernel(rows, cols, count, joined, divisor, tiles, out, own, scaled, acc):
    width = own.shape[0]
    for block in range(NBLK):
        group, place = divmod(block, 4)
        span = slice((4 + place) * 32, (5 + place) * 32)
        own_path, neigh_path = (
            joined[4 * group + path, span].astype(jnp.float32)
            + joined[4 * group + 2 + path, span].astype(jnp.float32)
            for path in range(2)
        )
        scaled[block] = (neigh_path / divisor[block : block + 1]).astype(jnp.bfloat16)
        acc[block] = own_path
    acc[NBLK:] = jnp.zeros((acc.shape[0] - NBLK, width, BLK), jnp.float32)
    live = count[0]
    spare = acc.shape[0] - 1

    def step(group, carry):
        for inner in range(UNROLL):
            slot = group * UNROLL + inner
            alive = slot < live
            source = jnp.where(alive, rows[0, slot], 0)
            target = jnp.where(alive, cols[0, slot], spare)
            acc[target] += jnp.dot(scaled[source], tiles[slot], preferred_element_type=jnp.float32)
        return carry

    lax.fori_loop(0, (live + UNROLL - 1) // UNROLL, step, 0)
    for block in range(NBLK):
        own[:, block * BLK : (block + 1) * BLK] = acc[block]
    for slot in range(out.shape[0] * CAP):
        part, place = divmod(slot, CAP)
        out[part, :, place * BLK : (place + 1) * BLK] = acc[NBLK + slot].astype(jnp.bfloat16)
    for part in range(out.shape[0]):
        path, half, place = part // 8, part // 4 % 2, part % 4
        span = slice(place * 32, (place + 1) * 32)
        total = joined[2 * half + path, span].astype(jnp.float32)
        for group in range(1, joined.shape[0] // 4):
            total += joined[4 * group + 2 * half + path, span].astype(jnp.float32)
        out[part, :, CAP * BLK :] = total.astype(jnp.bfloat16)


def layer_kernel(joined, out):
    for peer in range(joined.shape[0]):
        half = peer // 2 % 2
        first = 4 * (peer // 4) + 2 * (peer % 2)
        for place in range(2):
            out[half * 16 : (half + 1) * 16, (first + place) * BLK : (first + place + 1) * BLK] = (
                joined[peer, SIDE + 16 * place : SIDE + 16 * (place + 1)]
            )


def piece_kernel(terms, extra, out, *, scale):
    total = terms[0, :, CAP * BLK :].astype(jnp.float32)
    for part in range(1, terms.shape[0]):
        total += terms[part, :, CAP * BLK :].astype(jnp.float32)
    total = (total * scale).astype(jnp.bfloat16)
    for part in range(out.shape[0]):
        out[part, : total.shape[0]] = total
        out[part, total.shape[0] :] = extra[...]


def collect_kernel(sends, own, returned, out, acc):
    acc[...] = own[...]
    for part in range(returned.shape[0]):
        for place in range(CAP):
            spot = lanes(sends[0, place, part])
            acc[:, spot] += returned[part, :, place * BLK : (place + 1) * BLK].astype(jnp.float32)
    out[...] = acc[...].astype(jnp.bfloat16)


def finish_kernel(chunks, grad_self, grad_neigh):
    width = grad_self.shape[0]
    order = interleave()
    for path, out in enumerate((grad_self, grad_neigh)):
        for place in range(4):
            pair = jnp.concatenate(
                [chunks[8 * path + 4 * half + place, :width] for half in range(2)], axis=1
            )
            out[:, 2 * place * BLK : 2 * (place + 1) * BLK] = lax.dot_general(
                pair, order, (((1,), (1,)), ((), ())), preferred_element_type=jnp.float32
            )


def whole(*shape):
    return pl.BlockSpec(shape, lambda *_: (0,) * len(shape))


def near(array):
    return pltpu.with_memory_space_constraint(array, pltpu.MemorySpace.VMEM)


def part_of(shape, *index):
    return pl.BlockSpec(shape, lambda *_: index)


def pieces(values):
    high = lax.reduce_precision(values, 8, 7)
    rest = values - high
    middle = lax.reduce_precision(rest, 8, 7)
    low = rest - middle
    return jnp.stack([high, middle, low], axis=-1).astype(jnp.bfloat16)


def gelu_and_slope(v):
    root = 0.7978845608028654
    t = jnp.tanh(root * (v + 0.044715 * v * v * v))
    value = 0.5 * v * (1.0 + t)
    slope = 0.5 * (1.0 + t) + 0.5 * v * (1.0 - t * t) * (root * (1.0 + 3 * 0.044715 * v * v))
    return value, slope


def swap(values, axis):
    return lax.all_to_all(values, axis, split_axis=0, concat_axis=0, tiled=True)


def per_device(
    node_feats,
    out_cotangent,
    weight_self,
    weight_neigh,
    out_bias,
    send_blocks,
    tile_rows,
    tile_cols,
    tile_count,
    tile_values,
):
    f32, bf16 = jnp.float32, jnp.bfloat16
    width = node_feats.shape[0]
    parts = lax.axis_size("dom")
    shards = lax.axis_size("feat")
    dims = width * shards
    outs = dims // 2
    send_blocks = jnp.transpose(send_blocks, (0, 2, 1))
    core = (lax.axis_index("feat") % 2).astype(jnp.int32).reshape(1)
    tiles = near(tile_values[0])

    outgoing = pl.pallas_call(
        outgoing_kernel,
        out_shape=jax.ShapeDtypeStruct((parts, width, CAP * BLK), bf16),
        in_specs=[SMEM, VMEM],
        out_specs=VMEM,
        compiler_params=PARAMS,
        name="outgoing",
    )(send_blocks, node_feats)
    halo = swap(outgoing, "dom")

    bias = jnp.pad(pieces(out_bias), ((0, 0), (0, BLK - 3)))
    packed = pl.pallas_call(
        pack_kernel,
        out_shape=HBM((shards, HEIGHT, BLK), bf16),
        grid=(1,),
        in_specs=[whole(width, dims), whole(width, dims), whole(width, ROWS), whole(width, BLK)],
        out_specs=whole(shards, HEIGHT, BLK),
        compiler_params=PARAMS,
        name="pack",
    )(weight_self, weight_neigh, out_cotangent, bias)

    packed, divisor = pl.pallas_call(
        aggregate_kernel,
        out_shape=(
            HBM((shards, HEIGHT, BLK), bf16),
            pltpu.VMEM((NBLK, BLK), f32),
        ),
        grid=(1,),
        in_specs=[
            SMEM,
            SMEM,
            SMEM,
            VMEM,
            VMEM,
            VMEM,
            pl.BlockSpec(memory_space=pl.ANY),
        ],
        out_specs=(part_of((shards, 4 * 32, BLK), 0, 1, 0), VMEM),
        scratch_shapes=[
            pltpu.VMEM((NBLK + parts * CAP, width + 16, BLK), bf16),
            pltpu.VMEM((NBLK + 1, width + 16, BLK), f32),
        ],
        input_output_aliases={6: 0},
        compiler_params=PARAMS,
        name="aggregate",
    )(tile_rows, tile_cols, tile_count, near(node_feats), near(halo), tiles, packed)
    packed = near(swap(packed, "feat"))

    weight, data, keep, send = pl.pallas_call(
        pre_kernel,
        out_shape=(
            pltpu.VMEM((dims, outs), bf16),
            pltpu.VMEM((dims, 4 * BLK), bf16),
            pltpu.VMEM((outs, 2 * BLK), f32),
            jax.ShapeDtypeStruct((outs, 2 * BLK), f32),
        ),
        in_specs=[SMEM, VMEM],
        out_specs=(VMEM,) * 4,
        compiler_params=PARAMS,
        name="pre",
    )(core, packed)
    received = lax.ppermute(send, "feat", PAIRS)
    layer, grad, local, sums = pl.pallas_call(
        slope_kernel,
        out_shape=(
            pltpu.VMEM((outs, 2 * BLK), bf16),
            jax.ShapeDtypeStruct((outs, 2 * BLK), bf16),
            pltpu.VMEM((outs, 2 * BLK), bf16),
            pltpu.VMEM((outs, BLK), bf16),
        ),
        in_specs=[VMEM, VMEM, VMEM],
        out_specs=(VMEM,) * 4,
        compiler_params=PARAMS,
        name="slope",
    )(near(keep), near(received), packed)
    other = lax.ppermute(grad, "feat", PAIRS)
    joined = pl.pallas_call(
        back_kernel,
        out_shape=jax.ShapeDtypeStruct((shards, HEIGHT, BLK), bf16),
        grid=(4,),
        in_specs=[SMEM, VMEM, VMEM, VMEM, VMEM, VMEM, VMEM],
        out_specs=pl.BlockSpec((shards // 4, HEIGHT, BLK), lambda i: (i, 0, 0)),
        scratch_shapes=[pltpu.VMEM((outs, 4 * BLK), bf16)],
        compiler_params=PARAMS,
        name="back",
    )(core, near(weight), near(data), near(local), near(other), near(layer), near(sums))
    joined = swap(joined, "feat")

    outgoing, own = pl.pallas_call(
        scatter_kernel,
        out_shape=(
            HBM((parts, width, (CAP + 1) * BLK), bf16),
            pltpu.VMEM((width, ROWS), f32),
        ),
        in_specs=[SMEM, SMEM, SMEM, VMEM, VMEM, VMEM],
        out_specs=(VMEM, VMEM),
        scratch_shapes=[
            pltpu.VMEM((NBLK, width, BLK), bf16),
            pltpu.VMEM((NBLK + parts * CAP + 1, width, BLK), f32),
        ],
        compiler_params=PARAMS,
        name="scatter",
    )(tile_rows, tile_cols, tile_count, near(joined), near(divisor), tiles)
    returned = near(swap(outgoing, "dom"))

    layer_out = pl.pallas_call(
        layer_kernel,
        out_shape=jax.ShapeDtypeStruct((width, ROWS), bf16),
        in_specs=[VMEM],
        out_specs=VMEM,
        compiler_params=PARAMS,
        name="layer",
    )(near(joined))
    bias_part = joined[:, TAIL:, :3].astype(f32).reshape(shards // 4, 2, 2, 16, 3)
    bias_part = jnp.sum(bias_part, axis=(0, 2, 4)).reshape(width)
    scale = 1.0 / float(ROWS * parts) ** 0.5
    extra = jnp.pad(pieces(bias_part * scale).T, ((0, 13), (0, BLK - width)))
    chunks = pl.pallas_call(
        functools.partial(piece_kernel, scale=scale),
        out_shape=HBM((parts, width + 16, BLK), bf16),
        in_specs=[VMEM, VMEM],
        out_specs=VMEM,
        compiler_params=PARAMS,
        name="piece",
    )(returned, near(extra))
    chunks = swap(chunks, "dom")
    feats_grad = pl.pallas_call(
        collect_kernel,
        out_shape=jax.ShapeDtypeStruct((width, ROWS), bf16),
        in_specs=[SMEM, VMEM, VMEM],
        out_specs=VMEM,
        scratch_shapes=[pltpu.VMEM((width, ROWS), f32)],
        compiler_params=PARAMS,
        name="collect",
    )(send_blocks, near(own), returned)
    grad_self, grad_neigh = pl.pallas_call(
        finish_kernel,
        out_shape=(jax.ShapeDtypeStruct((width, dims), f32),) * 2,
        in_specs=[VMEM],
        out_specs=(VMEM, VMEM),
        compiler_params=PARAMS,
        name="finish",
    )(near(chunks))
    grad_bias = jnp.sum(chunks[:, width : width + 3, :width].astype(f32), axis=(0, 1))
    return (layer_out, feats_grad, grad_self, grad_neigh, grad_bias)


def solution(mesh):
    in_specs = (
        P("feat", "dom"),
        P("feat", "dom"),
        P("feat", None),
        P("feat", None),
        P("feat"),
        P("dom", None, None),
        P("dom", None),
        P("dom", None),
        P("dom"),
        P("dom", None, None, None),
    )
    out_specs = (P("feat", "dom"), P("feat", "dom"), P("feat", None), P("feat", None), P("feat"))
    return jax.shard_map(
        per_device, mesh=mesh, in_specs=in_specs, out_specs=out_specs, check_vma=False
    )
```

```python
import functools

import jax
import jax.numpy as jnp
from jax import lax
from jax.experimental import pallas as pl
from jax.experimental.pallas import tpu as pltpu
from jax.sharding import PartitionSpec as P

BLK = 128
NBLK = 32
CAP = 2
TMAX = 64
ROWS = 4096
UNROLL = 8

SMEM = pl.BlockSpec(memory_space=pltpu.SMEM)
HBM = pltpu.MemorySpace.HBM
VMEM = pl.BlockSpec(memory_space=pltpu.VMEM)
PARAMS = pltpu.CompilerParams(vmem_limit_bytes=32 << 20)
PAIRS = [(i, i ^ 1) for i in range(32)]


def lanes(block):
    return pl.ds(pl.multiple_of(block * BLK, BLK), BLK)


def outgoing_kernel(sends, feats, out, sems):
    copies = []
    for part in range(out.shape[0]):
        for place in range(CAP):
            copies.append(
                pltpu.make_async_copy(
                    feats.at[:, lanes(sends[0, place, part])],
                    out.at[part, :, place * BLK : (place + 1) * BLK],
                    sems.at[part, place],
                )
            )
    for copy in copies:
        copy.start()
    for copy in copies:
        copy.wait()


SIDE = 8 * 32
TAIL = 9 * 32
HEIGHT = TAIL + 16


def interleave():
    lane = lax.broadcasted_iota(jnp.int32, (2 * BLK, 2 * BLK), 0)
    spot = lax.broadcasted_iota(jnp.int32, (2 * BLK, 2 * BLK), 1)
    goal = (lane % 32) // 16 * BLK + lane // 32 * 16 + lane % 16
    return jnp.where(goal == spot, 1.0, 0.0).astype(jnp.bfloat16)


def pack_kernel(weight_self, weight_neigh, cotangent, bias, out):
    order = interleave()
    for path, weight in enumerate((weight_self, weight_neigh)):
        for block in range(weight.shape[1] // (2 * BLK)):
            mixed = jnp.dot(
                weight[:, 2 * block * BLK : 2 * (block + 1) * BLK],
                order,
                preferred_element_type=jnp.float32,
            ).astype(jnp.bfloat16)
            for half in range(2):
                part = mixed[:, half * BLK : (half + 1) * BLK]
                for group in range(out.shape[0] // 4):
                    out[4 * group + 2 * half + path, block * 32 : (block + 1) * 32] = part
    for peer in range(out.shape[0]):
        half = peer // 2 % 2
        first = 4 * (peer // 4) + 2 * (peer % 2)
        rows = slice(half * 16, (half + 1) * 16)
        for place in range(2):
            out[peer, SIDE + 16 * place : SIDE + 16 * (place + 1)] = cotangent[
                rows, (first + place) * BLK : (first + place + 1) * BLK
            ]
        out[peer, TAIL:] = bias[rows]


def aggregate_kernel(rows, cols, count, feats, halo, tiles, packed, out, divisor, ext, acc):
    width = feats.shape[0]
    ones = jnp.ones((16, BLK), jnp.bfloat16)
    for block in range(NBLK):
        ext[block, :width] = feats[:, block * BLK : (block + 1) * BLK]
        ext[block, width:] = ones
    for slot in range(halo.shape[0] * CAP):
        part, place = divmod(slot, CAP)
        ext[NBLK + slot, :width] = halo[part, :, place * BLK : (place + 1) * BLK]
        ext[NBLK + slot, width:] = ones
    acc[...] = jnp.zeros_like(acc)
    live = count[0]

    def step(group, carry):
        for inner in range(UNROLL):
            slot = group * UNROLL + inner
            alive = slot < live
            source = jnp.where(alive, cols[0, slot], 0)
            target = jnp.where(alive, rows[0, slot], NBLK)
            acc[target] += lax.dot_general(
                ext[source], tiles[slot], (((1,), (1,)), ((), ())), preferred_element_type=jnp.float32
            )
        return carry

    lax.fori_loop(0, (live + UNROLL - 1) // UNROLL, step, 0)
    for block in range(NBLK):
        group, place = divmod(block, 4)
        span = slice(place * 32, (place + 1) * 32)
        div = jnp.maximum(acc[block, width : width + 1], 1.0)
        divisor[block : block + 1] = div
        mean = (acc[block, :width] / div).astype(jnp.bfloat16)
        for half in range(2):
            out[4 * group + 2 * half, span] = feats[:, block * BLK : (block + 1) * BLK]
            out[4 * group + 2 * half + 1, span] = mean


def pre_kernel(core, packed, weight, data, keep, send):
    dims, outs = weight.shape
    for block in range(4):
        span = slice(block * BLK, (block + 1) * BLK)
        weight[:, span] = packed[:, block * 32 : (block + 1) * 32].reshape(dims, BLK)
        data[:, span] = packed[:, (4 + block) * 32 : (5 + block) * 32].reshape(dims, BLK)
    even = core[0] == 0
    for start in range(0, outs, 2 * BLK):
        rows = slice(start, start + 2 * BLK)
        product = lax.dot_general(
            weight[:, rows], data[...], (((0,), (0,)), ((), ())), preferred_element_type=jnp.float32
        )
        first, second = product[:, : 2 * BLK], product[:, 2 * BLK :]
        keep[rows] = jnp.where(even, first, second)
        send[rows] = jnp.where(even, second, first)


def slope_kernel(keep, received, packed, layer, grad, local, sums):
    outs = keep.shape[0]
    bias = packed[:, TAIL:].reshape(outs, BLK).astype(jnp.float32)
    bias = jnp.sum(bias, axis=1, keepdims=True)
    total = jnp.zeros((outs, 1), jnp.float32)
    for place in range(2):
        span = slice(place * BLK, (place + 1) * BLK)
        cotangent = packed[:, SIDE + 16 * place : SIDE + 16 * (place + 1)].reshape(outs, BLK)
        value, slope = gelu_and_slope(keep[:, span] + received[:, span] + bias)
        layer[:, span] = value.astype(jnp.bfloat16)
        rounded = (cotangent.astype(jnp.float32) * slope).astype(jnp.bfloat16)
        grad[:, span] = rounded
        local[:, span] = rounded
        total += jnp.sum(rounded.astype(jnp.float32), axis=1, keepdims=True)
    high = total.astype(jnp.bfloat16).astype(jnp.float32)
    middle = (total - high).astype(jnp.bfloat16).astype(jnp.float32)
    low = total - high - middle
    lane = lax.broadcasted_iota(jnp.int32, (outs, BLK), 1)
    spread = jnp.where(lane == 0, high, jnp.where(lane == 1, middle, jnp.where(lane == 2, low, 0.0)))
    sums[...] = spread.astype(jnp.bfloat16)


def back_kernel(core, weight, data, grad, other, layer, sums, out, both):
    peers = out.shape[0]
    rows = pl.ds(pl.multiple_of(pl.program_id(0) * peers * 32, peers * 32), peers * 32)
    outs = pl.ds(pl.multiple_of(pl.program_id(0) * peers * 16, peers * 16), peers * 16)

    @pl.when(pl.program_id(0) == 0)
    def _():
        even = core[0] == 0
        both[:, : 2 * BLK] = jnp.where(even, grad[...], other[...])
        both[:, 2 * BLK :] = jnp.where(even, other[...], grad[...])

    term = lax.dot_general(
        data[rows], both[...], (((1,), (1,)), ((), ())), preferred_element_type=jnp.float32
    ).astype(jnp.bfloat16)
    back = jnp.dot(weight[rows], both[...], preferred_element_type=jnp.float32).astype(jnp.bfloat16)
    for block in range(4):
        span = slice(block * BLK, (block + 1) * BLK)
        out[:, block * 32 : (block + 1) * 32] = term[:, span].reshape(peers, 32, BLK)
        out[:, (4 + block) * 32 : (5 + block) * 32] = back[:, span].reshape(peers, 32, BLK)
    for place in range(2):
        value = layer[outs, place * BLK : (place + 1) * BLK]
        out[:, SIDE + 16 * place : SIDE + 16 * (place + 1)] = value.reshape(peers, 16, BLK)
    out[:, TAIL:] = sums[outs].reshape(peers, 16, BLK)


def scatter_kernel(rows, cols, count, joined, divisor, tiles, out, own, scaled, acc):
    width = own.shape[0]
    for block in range(NBLK):
        group, place = divmod(block, 4)
        span = slice((4 + place) * 32, (5 + place) * 32)
        own_path, neigh_path = (
            joined[4 * group + path, span].astype(jnp.float32)
            + joined[4 * group + 2 + path, span].astype(jnp.float32)
            for path in range(2)
        )
        scaled[block] = (neigh_path / divisor[block : block + 1]).astype(jnp.bfloat16)
        acc[block] = own_path
    acc[NBLK:] = jnp.zeros((acc.shape[0] - NBLK, width, BLK), jnp.float32)
    live = count[0]
    spare = acc.shape[0] - 1

    def step(group, carry):
        for inner in range(UNROLL):
            slot = group * UNROLL + inner
            alive = slot < live
            source = jnp.where(alive, rows[0, slot], 0)
            target = jnp.where(alive, cols[0, slot], spare)
            acc[target] += jnp.dot(scaled[source], tiles[slot], preferred_element_type=jnp.float32)
        return carry

    lax.fori_loop(0, (live + UNROLL - 1) // UNROLL, step, 0)
    for block in range(NBLK):
        own[:, block * BLK : (block + 1) * BLK] = acc[block]
    for slot in range(out.shape[0] * CAP):
        part, place = divmod(slot, CAP)
        out[part, :, place * BLK : (place + 1) * BLK] = acc[NBLK + slot].astype(jnp.bfloat16)
    for part in range(out.shape[0]):
        path, half, place = part // 8, part // 4 % 2, part % 4
        span = slice(place * 32, (place + 1) * 32)
        total = joined[2 * half + path, span].astype(jnp.float32)
        for group in range(1, joined.shape[0] // 4):
            total += joined[4 * group + 2 * half + path, span].astype(jnp.float32)
        out[part, :, CAP * BLK :] = total.astype(jnp.bfloat16)


def layer_kernel(joined, out):
    for peer in range(joined.shape[0]):
        half = peer // 2 % 2
        first = 4 * (peer // 4) + 2 * (peer % 2)
        for place in range(2):
            out[half * 16 : (half + 1) * 16, (first + place) * BLK : (first + place + 1) * BLK] = (
                joined[peer, SIDE + 16 * place : SIDE + 16 * (place + 1)]
            )


def piece_kernel(terms, extra, out, *, scale):
    total = terms[0, :, CAP * BLK :].astype(jnp.float32)
    for part in range(1, terms.shape[0]):
        total += terms[part, :, CAP * BLK :].astype(jnp.float32)
    total = (total * scale).astype(jnp.bfloat16)
    for part in range(out.shape[0]):
        out[part, : total.shape[0]] = total
        out[part, total.shape[0] :] = extra[...]


def collect_kernel(sends, own, returned, out, acc):
    acc[...] = own[...]
    for part in range(returned.shape[0]):
        for place in range(CAP):
            spot = lanes(sends[0, place, part])
            acc[:, spot] += returned[part, :, place * BLK : (place + 1) * BLK].astype(jnp.float32)
    out[...] = acc[...].astype(jnp.bfloat16)


def finish_kernel(chunks, grad_self, grad_neigh, grad_bias):
    width = grad_self.shape[0]
    order = interleave()
    for path, out in enumerate((grad_self, grad_neigh)):
        for place in range(4):
            pair = jnp.concatenate(
                [chunks[8 * path + 4 * half + place, :width] for half in range(2)], axis=1
            )
            out[:, 2 * place * BLK : 2 * (place + 1) * BLK] = lax.dot_general(
                pair, order, (((1,), (1,)), ((), ())), preferred_element_type=jnp.float32
            )
    total = chunks[0, width:].astype(jnp.float32)
    for part in range(1, chunks.shape[0]):
        total += chunks[part, width:].astype(jnp.float32)
    grad_bias[...] = jnp.sum(total, axis=0, keepdims=True)


def whole(*shape):
    return pl.BlockSpec(shape, lambda *_: (0,) * len(shape))


def near(array):
    return pltpu.with_memory_space_constraint(array, pltpu.MemorySpace.VMEM)


def far(array):
    return pltpu.with_memory_space_constraint(array, HBM)


def part_of(shape, *index):
    return pl.BlockSpec(shape, lambda *_: index)


def pieces(values):
    high = lax.reduce_precision(values, 8, 7)
    rest = values - high
    middle = lax.reduce_precision(rest, 8, 7)
    low = rest - middle
    return jnp.stack([high, middle, low], axis=-1).astype(jnp.bfloat16)


def gelu_and_slope(v):
    root = 0.7978845608028654
    t = jnp.tanh(root * (v + 0.044715 * v * v * v))
    value = 0.5 * v * (1.0 + t)
    slope = 0.5 * (1.0 + t) + 0.5 * v * (1.0 - t * t) * (root * (1.0 + 3 * 0.044715 * v * v))
    return value, slope


def swap(values, axis):
    return lax.all_to_all(values, axis, split_axis=0, concat_axis=0, tiled=True)


def per_device(
    node_feats,
    out_cotangent,
    weight_self,
    weight_neigh,
    out_bias,
    send_blocks,
    tile_rows,
    tile_cols,
    tile_count,
    tile_values,
):
    f32, bf16 = jnp.float32, jnp.bfloat16
    width = node_feats.shape[0]
    parts = lax.axis_size("dom")
    shards = lax.axis_size("feat")
    dims = width * shards
    outs = dims // 2
    send_blocks = jnp.transpose(send_blocks, (0, 2, 1))
    core = (lax.axis_index("feat") % 2).astype(jnp.int32).reshape(1)
    tiles = near(tile_values[0])

    outgoing = pl.pallas_call(
        outgoing_kernel,
        out_shape=HBM((parts, width, CAP * BLK), bf16),
        in_specs=[SMEM, pl.BlockSpec(memory_space=HBM)],
        out_specs=pl.BlockSpec(memory_space=HBM),
        scratch_shapes=[pltpu.SemaphoreType.DMA((parts, CAP))],
        compiler_params=PARAMS,
        name="outgoing",
    )(far(send_blocks), far(node_feats))
    halo = swap(outgoing, "dom")

    bias = jnp.pad(pieces(out_bias), ((0, 0), (0, BLK - 3)))
    packed = pl.pallas_call(
        pack_kernel,
        out_shape=HBM((shards, HEIGHT, BLK), bf16),
        grid=(1,),
        in_specs=[whole(width, dims), whole(width, dims), whole(width, ROWS), whole(width, BLK)],
        out_specs=whole(shards, HEIGHT, BLK),
        compiler_params=PARAMS,
        name="pack",
    )(weight_self, weight_neigh, out_cotangent, bias)

    packed, divisor = pl.pallas_call(
        aggregate_kernel,
        out_shape=(
            HBM((shards, HEIGHT, BLK), bf16),
            pltpu.VMEM((NBLK, BLK), f32),
        ),
        grid=(1,),
        in_specs=[
            SMEM,
            SMEM,
            SMEM,
            VMEM,
            VMEM,
            VMEM,
            pl.BlockSpec(memory_space=pl.ANY),
        ],
        out_specs=(part_of((shards, 4 * 32, BLK), 0, 1, 0), VMEM),
        scratch_shapes=[
            pltpu.VMEM((NBLK + parts * CAP, width + 16, BLK), bf16),
            pltpu.VMEM((NBLK + 1, width + 16, BLK), f32),
        ],
        input_output_aliases={6: 0},
        compiler_params=PARAMS,
        name="aggregate",
    )(tile_rows, tile_cols, tile_count, near(node_feats), near(halo), tiles, packed)
    packed = near(swap(packed, "feat"))

    weight, data, keep, send = pl.pallas_call(
        pre_kernel,
        out_shape=(
            pltpu.VMEM((dims, outs), bf16),
            pltpu.VMEM((dims, 4 * BLK), bf16),
            pltpu.VMEM((outs, 2 * BLK), f32),
            jax.ShapeDtypeStruct((outs, 2 * BLK), f32),
        ),
        in_specs=[SMEM, VMEM],
        out_specs=(VMEM,) * 4,
        compiler_params=PARAMS,
        name="pre",
    )(core, packed)
    received = lax.ppermute(send, "feat", PAIRS)
    layer, grad, local, sums = pl.pallas_call(
        slope_kernel,
        out_shape=(
            pltpu.VMEM((outs, 2 * BLK), bf16),
            jax.ShapeDtypeStruct((outs, 2 * BLK), bf16),
            pltpu.VMEM((outs, 2 * BLK), bf16),
            pltpu.VMEM((outs, BLK), bf16),
        ),
        in_specs=[VMEM, VMEM, VMEM],
        out_specs=(VMEM,) * 4,
        compiler_params=PARAMS,
        name="slope",
    )(near(keep), near(received), packed)
    other = lax.ppermute(grad, "feat", PAIRS)
    joined = pl.pallas_call(
        back_kernel,
        out_shape=jax.ShapeDtypeStruct((shards, HEIGHT, BLK), bf16),
        grid=(4,),
        in_specs=[SMEM, VMEM, VMEM, VMEM, VMEM, VMEM, VMEM],
        out_specs=pl.BlockSpec((shards // 4, HEIGHT, BLK), lambda i: (i, 0, 0)),
        scratch_shapes=[pltpu.VMEM((outs, 4 * BLK), bf16)],
        compiler_params=PARAMS,
        name="back",
    )(core, near(weight), near(data), near(local), near(other), near(layer), near(sums))
    joined = swap(joined, "feat")

    outgoing, own = pl.pallas_call(
        scatter_kernel,
        out_shape=(
            HBM((parts, width, (CAP + 1) * BLK), bf16),
            HBM((width, ROWS), f32),
        ),
        in_specs=[SMEM, SMEM, SMEM, VMEM, VMEM, VMEM],
        out_specs=(VMEM, VMEM),
        scratch_shapes=[
            pltpu.VMEM((NBLK, width, BLK), bf16),
            pltpu.VMEM((NBLK + parts * CAP + 1, width, BLK), f32),
        ],
        compiler_params=PARAMS,
        name="scatter",
    )(tile_rows, tile_cols, tile_count, near(joined), near(divisor), tiles)
    returned = near(swap(outgoing, "dom"))

    layer_out = pl.pallas_call(
        layer_kernel,
        out_shape=jax.ShapeDtypeStruct((width, ROWS), bf16),
        in_specs=[VMEM],
        out_specs=VMEM,
        compiler_params=PARAMS,
        name="layer",
    )(near(joined))
    bias_part = joined[:, TAIL:, :3].astype(f32).reshape(shards // 4, 2, 2, 16, 3)
    bias_part = jnp.sum(bias_part, axis=(0, 2, 4)).reshape(width)
    scale = 1.0 / float(ROWS * parts) ** 0.5
    extra = jnp.pad(pieces(bias_part * scale).T, ((0, 5), (0, BLK - width)))
    chunks = pl.pallas_call(
        functools.partial(piece_kernel, scale=scale),
        out_shape=HBM((parts, width + 8, BLK), bf16),
        in_specs=[VMEM, VMEM],
        out_specs=VMEM,
        compiler_params=PARAMS,
        name="piece",
    )(returned, near(extra))
    chunks = swap(chunks, "dom")
    feats_grad = pl.pallas_call(
        collect_kernel,
        out_shape=jax.ShapeDtypeStruct((width, ROWS), bf16),
        in_specs=[SMEM, VMEM, VMEM],
        out_specs=VMEM,
        scratch_shapes=[pltpu.VMEM((width, ROWS), f32)],
        compiler_params=PARAMS,
        name="collect",
    )(send_blocks, near(own), returned)
    grad_self, grad_neigh, grad_bias = pl.pallas_call(
        finish_kernel,
        out_shape=(jax.ShapeDtypeStruct((width, dims), f32),) * 2
        + (jax.ShapeDtypeStruct((1, BLK), f32),),
        in_specs=[VMEM],
        out_specs=(VMEM,) * 3,
        compiler_params=PARAMS,
        name="finish",
    )(near(chunks))
    grad_bias = grad_bias[0, :width]
    return (layer_out, feats_grad, grad_self, grad_neigh, grad_bias)


def solution(mesh):
    in_specs = (
        P("feat", "dom"),
        P("feat", "dom"),
        P("feat", None),
        P("feat", None),
        P("feat"),
        P("dom", None, None),
        P("dom", None),
        P("dom", None),
        P("dom"),
        P("dom", None, None, None),
    )
    out_specs = (P("feat", "dom"), P("feat", "dom"), P("feat", None), P("feat", None), P("feat"))
    return jax.shard_map(
        per_device, mesh=mesh, in_specs=in_specs, out_specs=out_specs, check_vma=False
    )
```
